32 devices in a mesh: basin: 2 (over x), pair: 8 (over z, y), row: 2 (over core).
Axes of the slice: x: 2, y: 2, z: 4, core: 2. Of those that a mesh axis runs over, the one named last changes fastest.
Arguments:
- snapshots: float32 [8192, 4096], P(('basin', 'row'), 'pair'), parts along dimension 0, may hold values from -60 to 60, as said below
- plan: int32 [4, 16], replicated, may hold values from 0 to 15, as said below
Outputs:
- rotated: float32 [8192, 4096], P(('basin', 'row'), 'pair'), parts along dimension 0
The draws below stay inside these ranges and needn't reach their ends.
There are 2 independent parts, one for each index of `basin`. The reference program is written for one: setup_inputs(seed, part) draws one part's arguments, and reference() takes and returns one part's arrays. A program takes and returns all parts, laid end to end along the dimension named above; an argument that names none is the same for every part. Nothing has to cross between parts.
Inputs may be any that keep to these rules, and one draw needn't show every extreme that they name: `plan`: each row of the table is a permutation of the 16 slots. Slots 2d and 2d + 1 lie on the d-th index of pair; in every round each index sends one of its two blocks to index d + 1 and the other to index d - 1 (both modulo 8). `snapshots`: real values.
All inputs are finite; a program needn't handle non-finite values.
Results may differ from the reference program's by a relative error of at most 0.0003.
Values sent between devices are 32-bit elements; how exact they have to be, the bound alone decides.
A program may use at most 64 MiB of HBM per device.

```python
import jax
import jax.numpy as jnp
from jax import lax

B = 256
ROUNDS = 4
NS_ITERS = 6
NP = 8
M = 4096
NCOL = 4096


def draw_snapshots(key, part):
    key_rows = jax.random.fold_in(key, 11)
    key_cols = jax.random.fold_in(key, 12)
    key_vals = jax.random.fold_in(key, 13)
    col_scale = jnp.exp(jax.random.uniform(key_cols, (1, NCOL), jnp.float32, jnp.log(0.3), jnp.log(3.0)))
    row_scale = jnp.exp(jax.random.uniform(key_rows, (M, 1), jnp.float32, jnp.log(0.3), jnp.log(3.0)))
    noise = jax.random.truncated_normal(key_vals, -6.0, 6.0, (M, NCOL), jnp.float32)
    values = noise * row_scale * col_scale
    return values.astype(jnp.float32)


def draw_plan(key, part):
    key_bits = jax.random.fold_in(key, 21)
    key_order = jax.random.fold_in(key, 22)
    bits = jax.random.randint(key_bits, (ROUNDS, NP), 0, 2)
    order = jax.random.randint(key_order, (ROUNDS, NP), 0, 2)
    device = jnp.arange(NP)[None, :]
    before = jnp.roll(bits, 1, axis=1)
    after = jnp.roll(bits, -1, axis=1)
    from_below = 2 * ((device + NP - 1) % NP) + before
    from_above = 2 * ((device + 1) % NP) + 1 - after
    slot_zero = jnp.where(order == 0, from_below, from_above)
    slot_one = jnp.where(order == 0, from_above, from_below)
    return jnp.stack((slot_zero, slot_one), axis=2).reshape(ROUNDS, 2 * NP).astype(jnp.int32)


def setup_inputs(seed: int = 0, part: int = 0) -> dict:
    splits = jax.random.split(jax.random.key(seed), 3)
    own_keys = jax.random.split(jax.random.fold_in(splits[2], part), 3)
    return {
        "snapshots": draw_snapshots(jax.random.fold_in(jax.random.fold_in(splits[2], part), 71), part),
        "plan": draw_plan(jax.random.fold_in(splits[2], 71), part),
    }


epsilon = 1e-6


def reference(snapshots, plan):
    highest = lax.Precision.HIGHEST
    identity = jnp.eye(B, dtype=jnp.float32)
    field = snapshots
    for round_index in range(ROUNDS):
        blocks = field.reshape(M, NP, 2, B)
        first = blocks[:, :, 0, :]
        second = blocks[:, :, 1, :]
        cross = jnp.einsum("mpa,mpb->pab", first, second, precision=highest)
        norm_first = jnp.sum(first * first, axis=0)
        norm_second = jnp.sum(second * second, axis=0)
        coupling = cross / (norm_first[:, :, None] + norm_second[:, None, :] + epsilon)
        system = identity[None] + jnp.einsum("pab,pcb->pac", coupling, coupling, precision=highest)
        scale = 1.0 + jnp.sum(coupling * coupling, axis=(1, 2))
        inverse = identity[None] / scale[:, None, None]
        for sweep in range(NS_ITERS):
            product = jnp.einsum("pab,pbc->pac", system, inverse, precision=highest)
            inverse = jnp.einsum("pab,pbc->pac", inverse, 2.0 * identity[None] - product, precision=highest)
        lifted = first - jnp.einsum("mpb,pab->mpa", second, coupling, precision=highest)
        mixed = jnp.einsum("mpa,pac->mpc", lifted, inverse, precision=highest)
        new_first = 2.0 * mixed - first
        new_second = second + 2.0 * jnp.einsum("mpa,pab->mpb", mixed, coupling, precision=highest)
        stacked = jnp.stack((new_first, new_second), axis=2).reshape(M, 2 * NP, B)
        field = stacked[:, plan[round_index], :].reshape(M, NCOL)
    return field
```

```python
import jax
import jax.numpy as jnp
from jax import lax
from jax.sharding import PartitionSpec as P

NS_ITERS = 6


epsilon = 1e-06


def matmul(left, right, left_dim=1, right_dim=0):
    return lax.dot_general(
        left,
        right,
        (((left_dim,), (right_dim,)), ((), ())),
        precision=lax.Precision.HIGH,
        preferred_element_type=jnp.float32,
    )


def partial_gram(first, second):
    cross = matmul(first, second, 0, 0)
    norm_first = jnp.sum(first * first, axis=0)
    norm_second = jnp.sum(second * second, axis=0)
    return cross, jnp.stack((norm_first, norm_second))


def add_from(values, axis, perm):
    return tuple(v + lax.ppermute(v, axis, perm) for v in values)


def rotate(first, second, gram):
    cross, norms = gram
    identity = jnp.eye(first.shape[1], dtype=jnp.float32)
    coupling = cross / (norms[0][:, None] + norms[1][None, :] + epsilon)
    system = identity + matmul(coupling, coupling, 1, 1)
    inverse = identity / (1.0 + jnp.sum(coupling * coupling))
    for sweep in range(NS_ITERS):
        inverse = matmul(inverse, 2.0 * identity - matmul(system, inverse))
    lifted = first - matmul(second, coupling, 1, 1)
    mixed = matmul(lifted, inverse)
    return 2.0 * mixed - first, second + 2.0 * matmul(mixed, coupling)


def second_goes_up(layout, device, count):
    above = (device + 1) % count
    zero = lax.dynamic_index_in_dim(layout, 2 * above, 0, False)
    one = lax.dynamic_index_in_dim(layout, 2 * above + 1, 0, False)
    return (zero == 2 * device + 1) | (one == 2 * device + 1)


def zero_from_below(layout, device, count):
    source = lax.dynamic_index_in_dim(layout, 2 * device, 0, False)
    return source // 2 == (device + count - 1) % count


def up_down(first, second, layout, device, count):
    swap = second_goes_up(layout, device, count)
    return jnp.where(swap, second, first), jnp.where(swap, first, second)


def ordered(below, above, layout, device, count):
    keep = zero_from_below(layout, device, count)
    return jnp.where(keep, below, above), jnp.where(keep, above, below)


def per_device(snapshots, plan):
    rounds = plan.shape[0]
    width = snapshots.shape[1] // 2
    half = snapshots.shape[0] // 2
    count = lax.axis_size("pair")
    me = lax.axis_index("pair")
    even, odd = me // 2 * 2, me // 2 * 2 + 1
    is_odd = me % 2 == 1
    cores = lax.axis_size("row")
    rows_perm = [(i, (i + 1) % cores) for i in range(cores)]
    twins = [(i, i ^ 1) for i in range(count)]

    def evens(step):
        return [(i, (i + step) % count) for i in range(0, count, 2)]

    def odds(step):
        return [(i, (i + step) % count) for i in range(1, count, 2)]

    def move(value, perm):
        return lax.ppermute(value, "pair", perm)

    first, second = snapshots[:, :width], snapshots[:, width:]
    gram = add_from(partial_gram(first, second), "row", rows_perm)
    first, second = rotate(first, second, gram)
    up, down = up_down(first, second, plan[0], me, count)
    same = move(jnp.where(is_odd, up[half:], down[:half]), odds(2) + evens(-2))
    cross = move(jnp.where(is_odd, up[:half], down[half:]), odds(1) + evens(-1))
    twin = move(jnp.where(is_odd, down[:half], up[half:]), twins)
    even_pair = ordered(
        jnp.where(is_odd, same, cross), jnp.where(is_odd, down[half:], twin), plan[0], even, count
    )
    odd_pair = ordered(
        jnp.where(is_odd, twin, up[:half]), jnp.where(is_odd, cross, same), plan[0], odd, count
    )

    for r in range(1, rounds):
        layout = plan[r]
        moved = []
        for pair, at in ((even_pair, even), (odd_pair, odd)):
            gram = add_from(partial_gram(*pair), "row", rows_perm)
            gram = add_from(gram, "pair", twins)
            moved.append(up_down(*rotate(*pair, gram), layout, at, count))
        (even_up, even_down), (odd_up, odd_down) = moved
        if r < rounds - 1:
            from_above = move(even_down, evens(-2) + odds(-2))
            from_below = move(odd_up, evens(2) + odds(2))
            even_pair = ordered(from_below, odd_down, layout, even, count)
            odd_pair = ordered(even_up, from_above, layout, odd, count)

    same = move(jnp.where(is_odd, even_down, odd_up), evens(2) + odds(-2))
    cross = move(jnp.where(is_odd, odd_up, even_down), evens(-1) + odds(1))
    twin = move(jnp.where(is_odd, odd_down, even_up), twins)
    below_top = jnp.where(is_odd, twin, same)
    below_bottom = jnp.where(is_odd, even_up, cross)
    above_top = jnp.where(is_odd, cross, odd_down)
    above_bottom = jnp.where(is_odd, same, twin)
    keep = zero_from_below(plan[rounds - 1], me, count)
    first_top = jnp.where(keep, below_top, above_top)
    first_bottom = jnp.where(keep, below_bottom, above_bottom)
    second_top = jnp.where(keep, above_top, below_top)
    second_bottom = jnp.where(keep, above_bottom, below_bottom)
    return jnp.block([[first_top, second_top], [first_bottom, second_bottom]])


def solution(mesh):
    in_specs = (P(("basin", "row"), "pair"), P())
    out_specs = P(("basin", "row"), "pair")
    return jax.shard_map(
        per_device, mesh=mesh, in_specs=in_specs, out_specs=out_specs, check_vma=False
    )
```

```python
import jax
import jax.numpy as jnp
from jax import lax
from jax.sharding import PartitionSpec as P

NS_ITERS = 6


epsilon = 1e-06


def matmul(left, right, left_dim=1, right_dim=0):
    return lax.dot_general(
        left,
        right,
        (((left_dim,), (right_dim,)), ((), ())),
        precision=lax.Precision.HIGH,
        preferred_element_type=jnp.float32,
    )


def partial_gram(first, second):
    cross = matmul(first, second, 0, 0)
    norm_first = jnp.sum(first * first, axis=0)
    norm_second = jnp.sum(second * second, axis=0)
    return cross, jnp.stack((norm_first, norm_second))


def add_from(values, axis, perm):
    return tuple(v + lax.ppermute(v, axis, perm) for v in values)


def rotate(first, second, gram):
    cross, norms = gram
    identity = jnp.eye(first.shape[1], dtype=jnp.float32)
    coupling = cross / (norms[0][:, None] + norms[1][None, :] + epsilon)
    system = identity + matmul(coupling, coupling, 1, 1)
    inverse = identity / (1.0 + jnp.sum(coupling * coupling))
    for sweep in range(NS_ITERS):
        inverse = matmul(inverse, 2.0 * identity - matmul(system, inverse))
    lifted = first - matmul(second, coupling, 1, 1)
    mixed = matmul(lifted, inverse)
    return 2.0 * mixed - first, second + 2.0 * matmul(mixed, coupling)


def second_goes_up(layout, device, count):
    above = (device + 1) % count
    zero = lax.dynamic_index_in_dim(layout, 2 * above, 0, False)
    one = lax.dynamic_index_in_dim(layout, 2 * above + 1, 0, False)
    return (zero == 2 * device + 1) | (one == 2 * device + 1)


def zero_from_below(layout, device, count):
    source = lax.dynamic_index_in_dim(layout, 2 * device, 0, False)
    return source // 2 == (device + count - 1) % count


def up_down(first, second, layout, device, count):
    swap = second_goes_up(layout, device, count)
    return jnp.where(swap, second, first), jnp.where(swap, first, second)


def ordered(below, above, layout, device, count):
    keep = zero_from_below(layout, device, count)
    return jnp.where(keep, below, above), jnp.where(keep, above, below)


def per_device(snapshots, plan):
    rounds = plan.shape[0]
    width = snapshots.shape[1] // 2
    half = snapshots.shape[0] // 2
    count = lax.axis_size("pair")
    me = lax.axis_index("pair")
    even, odd = me // 2 * 2, me // 2 * 2 + 1
    is_odd = me % 2 == 1
    cores = lax.axis_size("row")
    rows_perm = [(i, (i + 1) % cores) for i in range(cores)]
    twins = [(i, i ^ 1) for i in range(count)]

    def evens(step):
        return [(i, (i + step) % count) for i in range(0, count, 2)]

    def odds(step):
        return [(i, (i + step) % count) for i in range(1, count, 2)]

    def move(value, perm):
        return lax.ppermute(value, "pair", perm)

    first, second = snapshots[:, :width], snapshots[:, width:]
    gram = add_from(partial_gram(first, second), "row", rows_perm)
    first, second = rotate(first, second, gram)
    up, down = up_down(first, second, plan[0], me, count)
    same = move(jnp.where(is_odd, up[half:], down[:half]), odds(2) + evens(-2))
    cross = move(jnp.where(is_odd, up[:half], down[half:]), odds(1) + evens(-1))
    twin = move(jnp.where(is_odd, down[:half], up[half:]), twins)
    even_pair = jnp.where(is_odd, same, cross), jnp.where(is_odd, down[half:], twin)
    odd_pair = jnp.where(is_odd, twin, up[:half]), jnp.where(is_odd, cross, same)

    pairs = [even_pair, odd_pair]
    previous = ()
    for r in range(1, rounds):
        layout = plan[r]
        moved = [None, None]
        for which in (0, 1) if r % 2 else (1, 0):
            pair, previous = lax.optimization_barrier((pairs[which], previous))
            pair = ordered(*pair, plan[r - 1], (even, odd)[which], count)
            gram = add_from(partial_gram(*pair), "row", rows_perm)
            gram = add_from(gram, "pair", twins)
            previous = up_down(*rotate(*pair, gram), layout, (even, odd)[which], count)
            moved[which] = previous
        (even_up, even_down), (odd_up, odd_down) = moved
        if r < rounds - 1:
            from_above = move(even_down, evens(-2) + odds(-2))
            from_below = move(odd_up, evens(2) + odds(2))
            pairs = [(from_below, odd_down), (even_up, from_above)]

    same = move(jnp.where(is_odd, even_down, odd_up), evens(2) + odds(-2))
    cross = move(jnp.where(is_odd, odd_up, even_down), evens(-1) + odds(1))
    twin = move(jnp.where(is_odd, odd_down, even_up), twins)
    below_top = jnp.where(is_odd, twin, same)
    below_bottom = jnp.where(is_odd, even_up, cross)
    above_top = jnp.where(is_odd, cross, odd_down)
    above_bottom = jnp.where(is_odd, same, twin)
    keep = zero_from_below(plan[rounds - 1], me, count)
    first_top = jnp.where(keep, below_top, above_top)
    first_bottom = jnp.where(keep, below_bottom, above_bottom)
    second_top = jnp.where(keep, above_top, below_top)
    second_bottom = jnp.where(keep, above_bottom, below_bottom)
    return jnp.block([[first_top, second_top], [first_bottom, second_bottom]])


def solution(mesh):
    in_specs = (P(("basin", "row"), "pair"), P())
    out_specs = P(("basin", "row"), "pair")
    return jax.shard_map(
        per_device, mesh=mesh, in_specs=in_specs, out_specs=out_specs, check_vma=False
    )
```

```python
import jax
import jax.numpy as jnp
from jax import lax
from jax.sharding import PartitionSpec as P

NS_ITERS = 6


epsilon = 1e-06


def matmul(left, right, left_dim=1, right_dim=0):
    return lax.dot_general(
        left,
        right,
        (((left_dim,), (right_dim,)), ((), ())),
        precision=lax.Precision.HIGH,
        preferred_element_type=jnp.float32,
    )


def partial_gram(first, second):
    cross = matmul(first, second, 0, 0)
    norm_first = jnp.sum(first * first, axis=0)
    norm_second = jnp.sum(second * second, axis=0)
    return cross, jnp.stack((norm_first, norm_second))


def add_from(values, axis, perm):
    return tuple(v + lax.ppermute(v, axis, perm) for v in values)


def rotate(first, second, gram):
    cross, norms = gram
    identity = jnp.eye(first.shape[1], dtype=jnp.float32)
    coupling = cross / (norms[0][:, None] + norms[1][None, :] + epsilon)
    system = identity + matmul(coupling, coupling, 1, 1)
    inverse = identity / (1.0 + jnp.sum(coupling * coupling))
    for sweep in range(NS_ITERS):
        inverse = matmul(inverse, 2.0 * identity - matmul(system, inverse))
    lifted = first - matmul(second, coupling, 1, 1)
    mixed = matmul(lifted, inverse)
    return 2.0 * mixed - first, second + 2.0 * matmul(mixed, coupling)


def second_goes_up(layout, device, count):
    above = (device + 1) % count
    zero = lax.dynamic_index_in_dim(layout, 2 * above, 0, False)
    one = lax.dynamic_index_in_dim(layout, 2 * above + 1, 0, False)
    return (zero == 2 * device + 1) | (one == 2 * device + 1)


def zero_from_below(layout, device, count):
    source = lax.dynamic_index_in_dim(layout, 2 * device, 0, False)
    return source // 2 == (device + count - 1) % count


def up_down(first, second, layout, device, count):
    swap = second_goes_up(layout, device, count)
    return jnp.where(swap, second, first), jnp.where(swap, first, second)


def ordered(below, above, layout, device, count):
    keep = zero_from_below(layout, device, count)
    return jnp.where(keep, below, above), jnp.where(keep, above, below)


def per_device(snapshots, plan):
    rounds = plan.shape[0]
    width = snapshots.shape[1] // 2
    half = snapshots.shape[0] // 2
    count = lax.axis_size("pair")
    me = lax.axis_index("pair")
    even, odd = me // 2 * 2, me // 2 * 2 + 1
    is_odd = me % 2 == 1
    cores = lax.axis_size("row")
    rows_perm = [(i, (i + 1) % cores) for i in range(cores)]
    twins = [(i, i ^ 1) for i in range(count)]

    def evens(step):
        return [(i, (i + step) % count) for i in range(0, count, 2)]

    def odds(step):
        return [(i, (i + step) % count) for i in range(1, count, 2)]

    def move(value, perm):
        return lax.ppermute(value, "pair", perm)

    first, second = snapshots[:, :width], snapshots[:, width:]
    gram = add_from(partial_gram(first, second), "row", rows_perm)
    first, second = rotate(first, second, gram)
    up, down = up_down(first, second, plan[0], me, count)
    same = move(jnp.where(is_odd, up[half:], down[:half]), odds(2) + evens(-2))
    cross = move(jnp.where(is_odd, up[:half], down[half:]), odds(1) + evens(-1))
    twin = move(jnp.where(is_odd, down[:half], up[half:]), twins)
    even_pair = jnp.where(is_odd, same, cross), jnp.where(is_odd, down[half:], twin)
    odd_pair = jnp.where(is_odd, twin, up[:half]), jnp.where(is_odd, cross, same)

    pairs = [even_pair, odd_pair]
    previous, pending, waiting = (), [], []
    for r in range(1, rounds):
        layout = plan[r]
        moved, sent = [None, None], [None, None]
        for which in (0, 1) if r % 2 else (1, 0):
            pair, previous = lax.optimization_barrier((pairs[which], previous))
            pair = tuple(jnp.concatenate(v) if isinstance(v, list) else v for v in pair)
            pair = ordered(*pair, plan[r - 1], (even, odd)[which], count)
            gram = add_from(partial_gram(*pair), "row", rows_perm)
            gram = add_from(gram, "pair", twins)
            gram, pending = lax.optimization_barrier((gram, pending))
            waiting[:1] = pending
            previous = up_down(*rotate(*pair, gram), layout, (even, odd)[which], count)
            moved[which] = previous
            up, down = previous
            waiting, pending = [], []
            if r < rounds - 1:
                value, perm = (up, evens(2) + odds(2)) if which else (down, evens(-2) + odds(-2))
                waiting = [move(value[: half // 2], perm), move(value[half // 2 :], perm)]
                pending = waiting[:1]
            sent[which] = waiting
        (even_up, even_down), (odd_up, odd_down) = moved
        if r < rounds - 1:
            pairs = [(sent[1], odd_down), (even_up, sent[0])]

    same = move(jnp.where(is_odd, even_down, odd_up), evens(2) + odds(-2))
    cross = move(jnp.where(is_odd, odd_up, even_down), evens(-1) + odds(1))
    twin = move(jnp.where(is_odd, odd_down, even_up), twins)
    below_top = jnp.where(is_odd, twin, same)
    below_bottom = jnp.where(is_odd, even_up, cross)
    above_top = jnp.where(is_odd, cross, odd_down)
    above_bottom = jnp.where(is_odd, same, twin)
    keep = zero_from_below(plan[rounds - 1], me, count)
    first_top = jnp.where(keep, below_top, above_top)
    first_bottom = jnp.where(keep, below_bottom, above_bottom)
    second_top = jnp.where(keep, above_top, below_top)
    second_bottom = jnp.where(keep, above_bottom, below_bottom)
    return jnp.block([[first_top, second_top], [first_bottom, second_bottom]])


def solution(mesh):
    in_specs = (P(("basin", "row"), "pair"), P())
    out_specs = P(("basin", "row"), "pair")
    return jax.shard_map(
        per_device, mesh=mesh, in_specs=in_specs, out_specs=out_specs, check_vma=False
    )
```

```python
import jax
import jax.numpy as jnp
from jax import lax
from jax.sharding import PartitionSpec as P

NS_ITERS = 6


epsilon = 1e-06


def matmul(left, right, left_dim=1, right_dim=0):
    return lax.dot_general(
        left,
        right,
        (((left_dim,), (right_dim,)), ((), ())),
        precision=lax.Precision.HIGH,
        preferred_element_type=jnp.float32,
    )


def partial_gram(first, second):
    cross = matmul(first, second, 0, 0)
    norm_first = jnp.sum(first * first, axis=0)
    norm_second = jnp.sum(second * second, axis=0)
    return jnp.concatenate((cross, norm_first[None], norm_second[None]))


def add_from(value, axis, perm):
    return value + lax.ppermute(value, axis, perm)


def rotate(first, second, gram):
    cross, norms = gram[:-2], gram[-2:]
    identity = jnp.eye(first.shape[1], dtype=jnp.float32)
    coupling = cross / (norms[0][:, None] + norms[1][None, :] + epsilon)
    system = identity + matmul(coupling, coupling, 1, 1)
    inverse = identity / (1.0 + jnp.sum(coupling * coupling))
    for sweep in range(NS_ITERS):
        inverse = matmul(inverse, 2.0 * identity - matmul(system, inverse))
    lifted = first - matmul(second, coupling, 1, 1)
    mixed = matmul(lifted, inverse)
    return 2.0 * mixed - first, second + 2.0 * matmul(mixed, coupling)


def second_goes_up(layout, device, count):
    above = (device + 1) % count
    zero = lax.dynamic_index_in_dim(layout, 2 * above, 0, False)
    one = lax.dynamic_index_in_dim(layout, 2 * above + 1, 0, False)
    return (zero == 2 * device + 1) | (one == 2 * device + 1)


def zero_from_below(layout, device, count):
    source = lax.dynamic_index_in_dim(layout, 2 * device, 0, False)
    return source // 2 == (device + count - 1) % count


def up_down(first, second, layout, device, count):
    swap = second_goes_up(layout, device, count)
    return jnp.where(swap, second, first), jnp.where(swap, first, second)


def ordered(below, above, layout, device, count):
    keep = zero_from_below(layout, device, count)
    return jnp.where(keep, below, above), jnp.where(keep, above, below)


def per_device(snapshots, plan):
    rounds = plan.shape[0]
    width = snapshots.shape[1] // 2
    half = snapshots.shape[0] // 2
    count = lax.axis_size("pair")
    me = lax.axis_index("pair")
    even, odd = me // 2 * 2, me // 2 * 2 + 1
    is_odd = me % 2 == 1
    cores = lax.axis_size("row")
    rows_perm = [(i, (i + 1) % cores) for i in range(cores)]
    twins = [(i, i ^ 1) for i in range(count)]

    def evens(step):
        return [(i, (i + step) % count) for i in range(0, count, 2)]

    def odds(step):
        return [(i, (i + step) % count) for i in range(1, count, 2)]

    def move(value, perm):
        return lax.ppermute(value, "pair", perm)

    first, second = snapshots[:, :width], snapshots[:, width:]
    gram = add_from(partial_gram(first, second), "row", rows_perm)
    first, second = rotate(first, second, gram)
    up, down = up_down(first, second, plan[0], me, count)
    same = move(jnp.where(is_odd, up[half:], down[:half]), odds(2) + evens(-2))
    cross = move(jnp.where(is_odd, up[:half], down[half:]), odds(1) + evens(-1))
    twin = move(jnp.where(is_odd, down[:half], up[half:]), twins)
    even_pair = jnp.where(is_odd, same, cross), jnp.where(is_odd, down[half:], twin)
    odd_pair = jnp.where(is_odd, twin, up[:half]), jnp.where(is_odd, cross, same)

    pairs = [even_pair, odd_pair]
    previous, pending, waiting = (), [], []
    for r in range(1, rounds):
        layout = plan[r]
        moved, sent = [None, None], [None, None]
        for which in (0, 1) if r % 2 else (1, 0):
            pair, previous = lax.optimization_barrier((pairs[which], previous))
            pair = tuple(jnp.concatenate(v) if isinstance(v, list) else v for v in pair)
            pair = ordered(*pair, plan[r - 1], (even, odd)[which], count)
            gram = add_from(partial_gram(*pair), "row", rows_perm)
            gram = add_from(gram, "pair", twins)
            gram, pending = lax.optimization_barrier((gram, pending))
            waiting[:1] = pending
            previous = up_down(*rotate(*pair, gram), layout, (even, odd)[which], count)
            moved[which] = previous
            up, down = previous
            waiting, pending = [], []
            if r < rounds - 1:
                value, perm = (up, evens(2) + odds(2)) if which else (down, evens(-2) + odds(-2))
                waiting = [move(value[: half // 2], perm), move(value[half // 2 :], perm)]
                pending = waiting[:1]
            sent[which] = waiting
        (even_up, even_down), (odd_up, odd_down) = moved
        if r < rounds - 1:
            pairs = [(sent[1], odd_down), (even_up, sent[0])]

    same = move(jnp.where(is_odd, even_down, odd_up), evens(2) + odds(-2))
    cross = move(jnp.where(is_odd, odd_up, even_down), evens(-1) + odds(1))
    twin = move(jnp.where(is_odd, odd_down, even_up), twins)
    below_top = jnp.where(is_odd, twin, same)
    below_bottom = jnp.where(is_odd, even_up, cross)
    above_top = jnp.where(is_odd, cross, odd_down)
    above_bottom = jnp.where(is_odd, same, twin)
    keep = zero_from_below(plan[rounds - 1], me, count)
    first_top = jnp.where(keep, below_top, above_top)
    first_bottom = jnp.where(keep, below_bottom, above_bottom)
    second_top = jnp.where(keep, above_top, below_top)
    second_bottom = jnp.where(keep, above_bottom, below_bottom)
    return jnp.block([[first_top, second_top], [first_bottom, second_bottom]])


def solution(mesh):
    in_specs = (P(("basin", "row"), "pair"), P())
    out_specs = P(("basin", "row"), "pair")
    return jax.shard_map(
        per_device, mesh=mesh, in_specs=in_specs, out_specs=out_specs, check_vma=False
    )
```
